128 devices in a mesh: pair: 16 (over y_hi, z, core), aux: 8 (over y_lo, x).
Axes of the slice: x: 4, y: 4 (y_hi: 2, y_lo: 2; y = y_hi * 2 + y_lo), z: 4, core: 2. Of those that a mesh axis runs over, the one named last changes fastest.
Arguments:
- c_occ: bfloat16 [12288, 1024], P('pair', 'aux'), may hold values from -0.1875 to 0.1875
- c_vir: bfloat16 [12288, 11264], P('pair', 'aux'), may hold values from -0.0546875 to 0.0546875
- e_occ: float32 [1024], P('aux'), may hold values from -2 to -0.3
- e_vir: float32 [11264], P('aux'), may hold values from 0.2 to 3
- tau_points: float32 [2], replicated, may hold values from 0.2 to 2
- pair_blocks: int32 [64, 2], P('pair'), may hold values from 0 to 767
- block_count: int32 [16], P('pair'), may hold values from 1 to 4, 40 in all
- three_center: bfloat16 [18432, 64, 256], P('aux', 'pair'), may hold values from -0.59765625 to 0.59765625
Outputs:
- coupling: float32 [18432, 2, 1024], P(('aux', 'pair'))
The draws below stay inside these ranges and needn't reach their ends.
Inputs may be any that keep to these rules, and one draw needn't show every extreme that they name: pair_blocks[s] names the AO shell blocks of the rows and the columns of slot s. Slots s with s mod 4 < block_count[s // 4] are live, the others are ignored; some index of pair has all 4 slots live.
All inputs are finite; a program needn't handle non-finite values. No bound on the sum of `block_count` on one device may be relied on, other than what follows from the above.
Results may differ from the reference program's by a relative error of at most 0.0046.
Values may be sent and summed in bfloat16 or wider, within the bound.
No kernel may reach another device: no remote copies, remote signals or barrier semaphores. Data moves between devices by JAX's collectives and lax.ppermute only.
A program may use at most 128 MiB of HBM per device.

```python
import math
import jax
import jax.numpy as jnp
import numpy as np
from jax import lax

BS = 16
NAO = 12288
NOCC = 1024
NVIR = 11264
AUX_DEV = 2304
K_DEV = 4
TAUS = 2
WIN_DEV = 128
NAUX = 18432
WIN = 1024
NBLK = 768
TOTAL_BLK = 64
N_PAIR = 16
N_AUX = 8


def touch_ends(result, own_key, least, largest):
    place = [jax.random.randint(jax.random.fold_in(own_key, axis), (), 0, length) for axis, length in enumerate(result.shape)]
    widest = result.shape.index(max(result.shape))
    next_to = place[:widest] + [(place[widest] + 1) % result.shape[widest]] + place[widest + 1:]
    return result.at[tuple(place)].set(least).at[tuple(next_to)].set(largest)


def raised(values, own_key, source, target, parts, factor):
    owner, partner = [(jnp.arange(values.shape[axis_at]) // (values.shape[axis_at] // parts)).reshape([-1 if axis == axis_at else 1 for axis in range(values.ndim)]) for axis_at in (source, target)]
    chosen = jax.random.permutation(own_key, parts)[partner]
    strong = (owner == chosen) | (owner == (partner + parts // 2) % parts)
    return jnp.where(strong, factor * values, values)


def level_of(rng, dims, split, low, high):
    def one(position, parts):
        heights = jax.random.uniform(jax.random.fold_in(jax.random.fold_in(rng, 6), position), (parts,), jnp.float32, low / len(split), high / len(split))
        return jnp.repeat(jnp.exp(heights), dims[position] // parts).reshape((-1,) + (1,) * (len(dims) - position - 1))

    gain = one(*split[0])
    for cut in split[1:]:
        gain = gain * one(*cut)
    return gain


def profile(count, total, bound, slope):
    portions = [(1 << 20) // math.isqrt(rank ** slope) + 1 for rank in range(2, count + 1)]
    surplus, given = total - bound - (count - 1), [1] * (count - 1)
    while surplus > 0:
        free = [i for i in range(count - 1) if given[i] < bound]
        whole, budget = sum([portions[i] for i in free]), surplus
        for i in free:
            extra = min(bound - given[i], max(1, budget * portions[i] // whole), surplus)
            given[i] = given[i] + extra
            surplus = surplus - extra
    return np.array([bound] + given)


def ragged_sizes(stream_key, count, total, bound, skew):
    if count == 2:
        one = jax.random.randint(stream_key, (), max(1, total - bound), min(bound, total - 1) + 1)
        return jnp.stack([one, total - one])
    sizes = jnp.asarray(profile(count, total, bound, skew), jnp.int32)
    couples = (count - 1) // 2
    giver, receiver = sizes[1:1 + 2 * couples:2], sizes[2:2 + 2 * couples:2]
    slack = jnp.minimum(giver - 1, bound - receiver)
    passed = jax.random.randint(jax.random.fold_in(stream_key, 1), (couples,), 0, 1 << 20) % (slack + 1)
    sizes = sizes.at[1:1 + 2 * couples:2].set(giver - passed).at[2:2 + 2 * couples:2].set(receiver + passed)
    return sizes[jax.random.permutation(jax.random.fold_in(stream_key, 2), count)]


def scatter_about(stream_key, shape, spread, most, shards=(), kind=jnp.bfloat16):
    entries = spread * jax.random.normal(stream_key, shape, jnp.float32)
    if shards:
        entries = entries * level_of(stream_key, shape, shards, -0.22, 0.18)
    return jnp.clip(entries, -most, most).astype(kind)


def noise_with(key, extent, spread, reach, cuts, heavy, held_as=jnp.bfloat16):
    result = spread * jax.random.normal(key, extent, jnp.float32)
    if cuts:
        result = result * level_of(key, extent, cuts, -0.22, 0.18)
    return jnp.clip(raised(result, jax.random.fold_in(key, 3), *heavy), -reach, reach).astype(held_as)


def setup_inputs(seed: int = 0) -> dict:
    keys = jax.random.split(jax.random.key(seed), 9)
    return {
        "c_occ": scatter_about(keys[0], (NAO, NOCC), NOCC ** -0.5, 0.1875, ((0, 16), (1, 8))),
        "c_vir": scatter_about(keys[1], (NAO, NVIR), NVIR ** -0.5, 0.0546875, ((0, 16), (1, 8))),
        "e_occ": jnp.clip(-2.0 + 1.7 * jax.random.uniform(keys[2], (NOCC,), jnp.float32) ** level_of(keys[2], (NOCC,), ((0, 8),), -0.2, 0.2), -2.0, -0.3),
        "e_vir": jnp.clip(0.2 + 2.8 * jax.random.uniform(keys[3], (NVIR,), jnp.float32) ** level_of(keys[3], (NVIR,), ((0, 8),), -0.2, 0.2), 0.2, 3.0),
        "tau_points": jnp.clip(jnp.exp(jax.random.uniform(keys[4], (TAUS,), jnp.float32, math.log(0.2), math.log(2.0))), 0.2, 2.0),
        "pair_blocks": touch_ends(jax.random.randint(keys[5], (TOTAL_BLK, 2), 0, NBLK), jax.random.fold_in(keys[5], 1), 0, NBLK - 1).astype(jnp.int32),
        "block_count": ragged_sizes(keys[6], N_PAIR, 5 * N_PAIR // 2, K_DEV, 2).astype(jnp.int32),
        "three_center": noise_with(keys[7], (NAUX, TOTAL_BLK, BS * BS), 0.1, 0.59765625, ((0, 8), (1, 16)), (1, 0, 16, 2.0)),
    }


def slot_rows(coefficient, energy, exponent_sign, tau_value, names):
    factor = jnp.exp(exponent_sign * tau_value * energy / 2.0)
    scaled = (coefficient.astype(jnp.float32) * factor[None, :]).astype(jnp.bfloat16)
    scaled = lax.optimization_barrier(scaled)
    blocks = scaled.reshape(NAO // BS, BS, coefficient.shape[1])
    return blocks[names].astype(jnp.float32)


def cross_tiles(rows):
    return jnp.einsum('sin,rjn->srij', rows, rows).astype(jnp.bfloat16)


def reference(c_occ, c_vir, e_occ, e_vir, tau_points, pair_blocks, block_count, three_center):
    occ_tiles = jnp.stack([cross_tiles(slot_rows(c_occ, e_occ, 1.0, tau_points[step], pair_blocks[:, 0])) for step in range(TAUS)])
    vir_tiles = jnp.stack([cross_tiles(slot_rows(c_vir, e_vir, -1.0, tau_points[step], pair_blocks[:, 1])) for step in range(TAUS)])
    slot_ids = jnp.arange(TOTAL_BLK, dtype=jnp.int32)
    live_mask = (slot_ids % K_DEV < block_count[slot_ids // K_DEV]).astype(jnp.float32)
    window = three_center.reshape(N_AUX, AUX_DEV, TOTAL_BLK, BS * BS)[:, :WIN_DEV]
    window = window.reshape(WIN, TOTAL_BLK, BS, BS).astype(jnp.float32)
    window = window * live_mask[None, :, None, None]
    occ_float = occ_tiles.astype(jnp.float32)
    vir_float = vir_tiles.astype(jnp.float32)

    def one_target(target):
        target = jnp.asarray(target).astype(jnp.int32)
        occ_row = lax.dynamic_index_in_dim(occ_float, target, 1, keepdims=False)
        vir_row = lax.dynamic_index_in_dim(vir_float, target, 1, keepdims=False)
        half_moved = jnp.einsum('tsij,psjl->tpsil', occ_row, window).astype(jnp.bfloat16)
        half_moved = lax.optimization_barrier(half_moved)
        summed = jnp.einsum('tpsil,tsml->tpim', half_moved.astype(jnp.float32), vir_row)
        summed = summed * lax.dynamic_index_in_dim(live_mask, target, 0, keepdims=False)
        return summed.astype(jnp.bfloat16).reshape(TAUS, WIN, BS * BS)

    moved = lax.map(one_target, slot_ids)
    moved = moved.reshape(N_PAIR, K_DEV, TAUS, WIN, BS * BS)

    def add_group(group, running):
        group = jnp.asarray(group).astype(jnp.int32)
        group_blocks = lax.dynamic_slice_in_dim(three_center, (group * K_DEV).astype(jnp.int32), K_DEV, 1)
        group_blocks = group_blocks.reshape(NAUX, K_DEV * BS * BS)
        right_side = lax.dynamic_index_in_dim(moved, group, 0, keepdims=False)
        right_side = right_side.transpose(1, 2, 0, 3).reshape(TAUS * WIN, K_DEV * BS * BS)
        return running + jnp.dot(group_blocks, right_side.T, preferred_element_type=jnp.float32)

    running = lax.fori_loop(0, N_PAIR, add_group, jnp.zeros((NAUX, TAUS * WIN), jnp.float32))
    return running.reshape(NAUX, TAUS, WIN)
```

```python
import numpy as np
import jax
import jax.numpy as jnp
from jax import lax
from jax.experimental import pallas as pl
from jax.experimental.pallas import tpu as pltpu
from jax.sharding import Mesh, PartitionSpec as P

BS = 16
TILE = BS * BS
WIN_DEV = 128
LIVE = 40
OWN = 4
CHIP = 2 * OWN
PAIR = ("yh", "z", "c")
ZY = ("yh", "z")
AUX = ("yl", "x")
SWAP = [(0, 1), (1, 0)]
XP = [(i, (i + 1) % 4) for i in range(4)]
XM = [(i, (i - 1) % 4) for i in range(4)]
F32 = jnp.float32
BF16 = jnp.bfloat16


def shift_zy(i):
    return [(y * 4 + z, ((y + i // 4) % 2) * 4 + (z + i % 4) % 4) for y in range(2) for z in range(4)]


def spread(x, axes, count):
    return lax.all_to_all(jnp.broadcast_to(x[None], (count,) + x.shape), axes, 0, 0)


def moved_kernel(where_ref, tiles_ref, win_ref, out_ref, acc_ref, eo_ref, ev_ref, oe_ref, ve_ref):
    lane = lax.broadcasted_iota(jnp.int32, (128, 2048), 1)
    row = lax.broadcasted_iota(jnp.int32, (128, 2048), 0)
    block = (lane // TILE) * BS
    eo_ref[...] = (row == block + (lane % TILE) // BS).astype(BF16)
    ev_ref[...] = (row == block + lane % BS).astype(BF16)
    acc_ref[...] = jnp.zeros_like(acc_ref)

    def group(g, carry):
        at = pl.multiple_of(g * 128, 128)
        occ = tiles_ref[:, 0, :, pl.ds(at, 128)].reshape(128, 128)
        vir = tiles_ref[:, 1, :, pl.ds(at, 128)].reshape(128, 128)
        oe_ref[...] = jnp.dot(occ, eo_ref[...], preferred_element_type=F32)
        ve_ref[...] = jnp.dot(vir, ev_ref[...], preferred_element_type=F32)
        wins = [win_ref[where_ref[g * 8 + r]] for r in range(8)]

        def target(s, c):
            rows = pl.multiple_of(s * BS, BS)
            total = acc_ref[pl.ds(pl.multiple_of(s * TILE, TILE), TILE), :]
            for r in range(8):
                o = oe_ref[pl.ds(rows, BS), r * TILE:(r + 1) * TILE]
                v = ve_ref[pl.ds(rows, BS), r * TILE:(r + 1) * TILE]
                kron = (o[:, None, :] * v[None, :, :]).astype(BF16).reshape(TILE, TILE)
                total = total + lax.dot_general(
                    kron, wins[r], (((1,), (1,)), ((), ())), preferred_element_type=F32)
            acc_ref[pl.ds(pl.multiple_of(s * TILE, TILE), TILE), :] = total
            return c

        return lax.fori_loop(0, CHIP, target, carry)

    lax.fori_loop(0, LIVE // 8, group, 0)
    out_ref[...] = acc_ref[...].astype(BF16)


def moved_blocks(where, tiles, windows):
    vm = pl.BlockSpec(memory_space=pltpu.VMEM)
    return pl.pallas_call(
        moved_kernel,
        out_shape=jax.ShapeDtypeStruct((CHIP * TILE, WIN_DEV), BF16),
        in_specs=[pl.BlockSpec(memory_space=pltpu.SMEM), vm, vm],
        out_specs=vm,
        scratch_shapes=[
            pltpu.VMEM((CHIP * TILE, WIN_DEV), F32),
            pltpu.VMEM((128, 2048), BF16),
            pltpu.VMEM((128, 2048), BF16),
            pltpu.VMEM((128, 2048), F32),
            pltpu.VMEM((128, 2048), F32),
        ],
        name="moved",
    )(where, tiles, windows)


def partial_kernel(dest_ref, place_ref, mine_ref, other_ref, *refs):
    out_ref = refs[-1]
    half = OWN * TILE
    tops = [ref[:half] for ref in refs[:6]] + [refs[6][...], refs[8][...]]
    bots = [ref[half:] for ref in refs[:6]] + [refs[7][...], refs[9][...]]
    for n in range(0, 8, 2):
        top = jnp.concatenate(tops[n:n + 2], axis=1)
        bot = jnp.concatenate(bots[n:n + 2], axis=1)
        value = jnp.dot(mine_ref[...], top, preferred_element_type=F32)
        value = value + jnp.dot(other_ref[...], bot, preferred_element_type=F32)
        for h in range(2):
            to = pl.multiple_of(place_ref[n + h] * WIN_DEV, WIN_DEV)
            out_ref[:, pl.ds(to, WIN_DEV)] = value[:, h * WIN_DEV:(h + 1) * WIN_DEV].astype(out_ref.dtype)


def partial_rows(dest, place, mine, other, pieces, dtype):
    rows = mine.shape[0] // 8
    cols = mine.shape[1]
    a_spec = pl.BlockSpec((rows, cols), lambda i, d, p: (d[0], 0))
    b_specs = [pl.BlockSpec(b.shape, lambda i, d, p: (0, 0)) for b in pieces]
    return pl.pallas_call(
        partial_kernel,
        out_shape=jax.ShapeDtypeStruct((rows, 8 * WIN_DEV), dtype),
        grid_spec=pltpu.PrefetchScalarGridSpec(
            num_scalar_prefetch=2,
            grid=(1,),
            in_specs=[a_spec, a_spec] + b_specs,
            out_specs=pl.BlockSpec((rows, 8 * WIN_DEV), lambda i, d, p: (0, 0)),
        ),
        name="partial",
    )(dest, place, mine, other, *pieces)


def per_device(c_occ, c_vir, e_occ, e_vir, tau_points, pair_blocks, block_count, three_center):
    y, z, c = lax.axis_index("yh"), lax.axis_index("z"), lax.axis_index("c")
    yl, x = lax.axis_index("yl"), lax.axis_index("x")
    group = (y * 4 + z) * 2 + c
    aux_rows = three_center.shape[0]
    chip_rows = aux_rows // 8

    window = jnp.transpose(three_center[:WIN_DEV], (1, 0, 2))
    gathered = [window] + [lax.ppermute(window, ZY, shift_zy(i)) for i in range(1, 8)]
    gathered = jnp.stack(gathered)
    windows = jnp.concatenate([gathered, lax.ppermute(gathered, "c", SWAP)])
    windows = windows.reshape(16 * OWN, WIN_DEV, TILE)

    mine = three_center.reshape(aux_rows, OWN * TILE)
    other = lax.ppermute(mine, "c", SWAP)

    facts = jnp.concatenate([pair_blocks.reshape(-1), block_count])
    facts = jnp.pad(facts, (0, 128 - facts.shape[0]))
    facts = spread(jnp.broadcast_to(facts[None], (8, 128)), PAIR, 16)[:, 0]
    names = facts[:, :2 * OWN].reshape(16 * OWN, 2)
    counts = facts[:, 2 * OWN]

    groups = jnp.arange(16, dtype=jnp.int32)
    before = jnp.sum(jnp.where(groups[None, :] < groups[:, None], counts[None, :], 0), axis=1)
    slots = jnp.arange(16 * OWN, dtype=jnp.int32)
    slot_in = slots % OWN
    slot_rank = jnp.where(
        slot_in < jnp.repeat(counts, OWN), jnp.repeat(before, OWN) + slot_in, -1)
    chosen = jnp.arange(LIVE, dtype=jnp.int32)[:, None] == slot_rank[None, :]
    sg = slots // OWN
    place_of = (
        jnp.where(sg % 2 == c, 0, 8 * OWN)
        + (((y - sg // 8) % 2) * 4 + (z - (sg // 2) % 4) % 4) * OWN + slot_in)
    where = jnp.sum(jnp.where(chosen, place_of[None, :], 0), axis=1)
    live_names = jnp.sum(jnp.where(chosen[:, :, None], names[None], 0), axis=1)

    local = jnp.arange(c_occ.shape[0], dtype=jnp.int32) - 0
    wanted = live_names[:, None, :] * BS + jnp.arange(BS, dtype=jnp.int32)[None, :, None]
    wanted = wanted.reshape(LIVE * BS, 2) - group * c_occ.shape[0]
    pick_occ = (wanted[:, :1] == local[None, :]).astype(BF16)
    pick_vir = (wanted[:, 1:] == local[None, :]).astype(BF16)
    rows = jnp.concatenate(
        [
            jnp.dot(pick_occ, c_occ, preferred_element_type=F32).astype(BF16),
            jnp.dot(pick_vir, c_vir, preferred_element_type=F32).astype(BF16),
        ], axis=1)
    n_occ = c_occ.shape[1]
    n_half = rows.shape[1] // 2
    kept = jnp.where(c == 0, rows[:, :n_half], rows[:, n_half:])
    given = jnp.where(c == 0, rows[:, n_half:], rows[:, :n_half])
    kept = kept + lax.ppermute(given, "c", SWAP)
    kept = lax.all_to_all(kept.reshape(8, -1, n_half), ZY, 0, 0)
    kept = jnp.sum(kept.astype(F32), axis=0).astype(BF16)
    kept = spread(kept, ZY, 8).reshape(LIVE * BS, n_half)
    given = lax.ppermute(kept, "c", SWAP)
    rows = jnp.concatenate(
        [jnp.where(c == 0, kept, given), jnp.where(c == 0, given, kept)], axis=1)

    tau = jnp.where(c == 0, tau_points[0], tau_points[1])
    factor = jnp.concatenate([jnp.exp(tau * e_occ / 2.0), jnp.exp(-tau * e_vir / 2.0)])
    scaled = (rows.astype(F32) * factor[None, :]).astype(BF16)
    padded = jnp.concatenate([scaled, jnp.zeros((OWN * BS, scaled.shape[1]), BF16)], axis=0)
    base_own = lax.dynamic_index_in_dim(before, group, 0, keepdims=False)
    base_next = lax.dynamic_index_in_dim(before, group + 1 - 2 * c, 0, keepdims=False)
    own = jnp.concatenate(
        [
            lax.dynamic_slice_in_dim(padded, base_own * BS, OWN * BS, 0),
            lax.dynamic_slice_in_dim(padded, base_next * BS, OWN * BS, 0),
        ], axis=0)
    numbers = (((1,), (1,)), ((), ()))
    grams = jnp.stack(
        [
            lax.dot_general(own[:, :n_occ], scaled[:, :n_occ], numbers, preferred_element_type=F32),
            lax.dot_general(own[:, n_occ:], scaled[:, n_occ:], numbers, preferred_element_type=F32),
        ])
    grams = grams.reshape(2, CHIP, BS, LIVE * BS).transpose(1, 0, 2, 3)
    grams = jnp.sum(lax.all_to_all(grams, AUX, 0, 0), axis=0)
    target = yl * 4 + x
    target_count = lax.dynamic_index_in_dim(
        counts, jnp.where(target < OWN, group, group + 1 - 2 * c), 0, keepdims=False)
    grams = jnp.where(target % OWN < target_count, grams, 0.0).astype(BF16)
    tiles = spread(grams, AUX, 8)

    moved = moved_blocks(where, tiles, windows)

    half = OWN * TILE
    by = lax.ppermute(moved, "yl", SWAP)
    bp = lax.ppermute(moved, "x", XP)
    bm = lax.ppermute(moved, "x", XM)
    byp = lax.ppermute(by, "x", XP)
    bym = lax.ppermute(by, "x", XM)
    pieces = [moved, by, bp, bm, byp, bym,
              lax.ppermute(bp[:half], "x", XP), lax.ppermute(bm[half:], "x", XM),
              lax.ppermute(byp[:half], "x", XP), lax.ppermute(bym[half:], "x", XM)]
    yo = 1 - yl
    xp, xm, x2 = (x - 1) % 4, (x + 1) % 4, (x + 2) % 4
    place = jnp.stack([yl * 4 + x, yo * 4 + x, yl * 4 + xp, yl * 4 + xm,
                       yo * 4 + xp, yo * 4 + xm, yl * 4 + x2, yo * 4 + x2]).astype(jnp.int32)

    received = []
    for i in (6, 2, 5, 7, 1, 3, 4):
        dest = (((y + i // 4) % 2) * 4 + (z + i % 4) % 4).astype(jnp.int32).reshape(1)
        part = partial_rows(dest, place, mine, other, pieces, BF16)
        received.append(lax.ppermute(part, ZY, shift_zy(i)))
    dest = (y * 4 + z).astype(jnp.int32).reshape(1)
    total = partial_rows(dest, place, mine, other, pieces, F32)
    for part in received:
        total = total + part.astype(F32)
    rows_dev = chip_rows // 2
    stay = jnp.where(c == 0, total[:rows_dev], total[rows_dev:])
    leave = jnp.where(c == 0, total[rows_dev:], total[:rows_dev])
    came = lax.ppermute(leave, "c", SWAP)
    return jnp.stack([jnp.where(c == 0, stay, came), jnp.where(c == 0, came, stay)], axis=1)


def solution(mesh):
    inner = Mesh(mesh.devices.reshape(2, 4, 2, 2, 4), ("yh", "z", "c", "yl", "x"))
    placed = (
        P(PAIR, AUX),
        P(PAIR, AUX),
        P(AUX),
        P(AUX),
        P(),
        P(PAIR, None),
        P(PAIR),
        P(AUX, PAIR, None),
    )
    return jax.shard_map(
        per_device,
        mesh=inner,
        in_specs=placed,
        out_specs=P(AUX + PAIR, None, None),
        check_vma=False,
    )
```

```python
import jax
import jax.numpy as jnp
from jax import lax
from jax.experimental import pallas as pl
from jax.experimental.pallas import tpu as pltpu
from jax.sharding import Mesh, PartitionSpec as P

BS = 16
TILE = BS * BS
WIN_DEV = 128
LIVE = 40
OWN = 4
CHIP = 2 * OWN
PAIR = ("yh", "z", "c")
ZY = ("yh", "z")
AUX = ("yl", "x")
SWAP = [(0, 1), (1, 0)]
XP = [(i, (i + 1) % 4) for i in range(4)]
XM = [(i, (i - 1) % 4) for i in range(4)]
F32 = jnp.float32
BF16 = jnp.bfloat16


def shift_zy(i):
    return [(y * 4 + z, ((y + i // 4) % 2) * 4 + (z + i % 4) % 4) for y in range(2) for z in range(4)]


def spread(x, axes, count):
    return lax.all_to_all(jnp.broadcast_to(x[None], (count,) + x.shape), axes, 0, 0)


def moved_kernel(where_ref, bound_ref, tiles_ref, *refs):
    pieces = refs[:16]
    out_ref, acc_ref, eo_ref, ev_ref, oe_ref, ve_ref, win_ref, all_ref, sems = refs[16:]
    copies = [
        pltpu.make_async_copy(piece, all_ref.at[pl.ds(n * OWN, OWN)], sems.at[n])
        for n, piece in enumerate(pieces)
    ]
    for copy in copies:
        copy.start()
    lane = lax.broadcasted_iota(jnp.int32, (128, 2048), 1)
    row = lax.broadcasted_iota(jnp.int32, (128, 2048), 0)
    block = (lane // TILE) * BS
    eo_ref[...] = (row == block + (lane % TILE) // BS).astype(BF16)
    ev_ref[...] = (row == block + lane % BS).astype(BF16)
    acc_ref[...] = jnp.zeros_like(acc_ref)
    for copy in copies:
        copy.wait()

    def group(g, carry):
        at = pl.multiple_of(g * 128, 128)
        occ = tiles_ref[:, 0, :, pl.ds(at, 128)].reshape(128, 128)
        vir = tiles_ref[:, 1, :, pl.ds(at, 128)].reshape(128, 128)
        oe_ref[...] = jnp.dot(occ, eo_ref[...], preferred_element_type=F32)
        ve_ref[...] = jnp.dot(vir, ev_ref[...], preferred_element_type=F32)
        for r in range(8):
            win_ref[r] = all_ref[where_ref[g * 8 + r]].T

        def target(s, c):
            rows = pl.multiple_of(s * BS, BS)
            to = pl.multiple_of(s * TILE, TILE)
            total = acc_ref[pl.ds(to, TILE), :]
            for r in range(8):
                v = ve_ref[pl.ds(rows, BS), r * TILE:(r + 1) * TILE]
                kron = jnp.concatenate(
                    [
                        (oe_ref[pl.ds(rows + i, 1), r * TILE:(r + 1) * TILE] * v).astype(BF16)
                        for i in range(BS)
                    ], axis=0)
                total = total + jnp.dot(kron, win_ref[r], preferred_element_type=F32)
            acc_ref[pl.ds(to, TILE), :] = total
            return c

        carry = lax.fori_loop(0, bound_ref[0], target, carry)
        return lax.fori_loop(OWN, OWN + bound_ref[1], target, carry)

    lax.fori_loop(0, LIVE // 8, group, 0)
    out_ref[...] = acc_ref[...].astype(BF16)


def moved_blocks(where, bounds, tiles, pieces):
    vm = pl.BlockSpec(memory_space=pltpu.VMEM)
    sm = pl.BlockSpec(memory_space=pltpu.SMEM)
    return pl.pallas_call(
        moved_kernel,
        out_shape=jax.ShapeDtypeStruct((CHIP * TILE, WIN_DEV), BF16),
        in_specs=[sm, sm, vm] + [pl.BlockSpec(memory_space=pl.ANY)] * 16,
        out_specs=vm,
        scratch_shapes=[
            pltpu.VMEM((CHIP * TILE, WIN_DEV), F32),
            pltpu.VMEM((128, 2048), BF16),
            pltpu.VMEM((128, 2048), BF16),
            pltpu.VMEM((128, 2048), F32),
            pltpu.VMEM((128, 2048), F32),
            pltpu.VMEM((8, TILE, WIN_DEV), BF16),
            pltpu.VMEM((16 * OWN, WIN_DEV, TILE), BF16),
            pltpu.SemaphoreType.DMA((16,)),
        ],
        name="moved",
    )(where, bounds, tiles, *pieces)


def partial_kernel(dest_ref, mine_ref, other_ref, *refs):
    half = OWN * TILE
    outs = refs[-8:]
    refs = list(refs[:-8])
    step = pl.program_id(0)
    tops = [ref[:half] for ref in refs]
    bots = [ref[half:] for ref in refs]
    values = []
    for n in range(0, len(tops), 2):
        top = jnp.concatenate(tops[n:n + 2], axis=1)
        bot = jnp.concatenate(bots[n:n + 2], axis=1)
        value = jnp.dot(mine_ref[...], top, preferred_element_type=F32)
        value = value + jnp.dot(other_ref[...], bot, preferred_element_type=F32)
        values.append(value.astype(BF16))
    value = jnp.concatenate(values, axis=1)
    rows = outs[0].shape[0]
    for k, out_ref in enumerate(outs):
        for h in range(2):
            @pl.when(dest_ref[k] == 2 * step + h)
            def _():
                out_ref[...] = value[h * rows:(h + 1) * rows]


def partial_rows(dests, mine, other, pieces):
    rows = mine.shape[0] // 8
    a_spec = pl.BlockSpec((2 * rows, mine.shape[1]), lambda i, d: (i, 0))
    vm = pl.BlockSpec(memory_space=pltpu.VMEM)
    return pl.pallas_call(
        partial_kernel,
        out_shape=[jax.ShapeDtypeStruct((rows, 4 * WIN_DEV), BF16)] * 8,
        grid_spec=pltpu.PrefetchScalarGridSpec(
            num_scalar_prefetch=1,
            grid=(4,),
            in_specs=[a_spec, a_spec] + [vm] * len(pieces),
            out_specs=[vm] * 8,
        ),
        name="partial",
    )(dests, mine, other, *pieces)


def finish_kernel(core_ref, place_ref, *refs):
    out_ref = refs[-1]
    first = core_ref[0] == 0
    for b in range(8):
        stay, came = refs[2 * (b // 4)], refs[2 * (b // 4) + 1]
        at = slice((b % 4) * WIN_DEV, (b % 4 + 1) * WIN_DEV)
        s, r = stay[:, at], came[:, at]
        to = pl.multiple_of(place_ref[b] * WIN_DEV, WIN_DEV)
        out_ref[:, 0, pl.ds(to, WIN_DEV)] = jnp.where(first, s, r)
        out_ref[:, 1, pl.ds(to, WIN_DEV)] = jnp.where(first, r, s)


def finish(core, place, parts):
    vm = pl.BlockSpec(memory_space=pltpu.VMEM)
    sm = pl.BlockSpec(memory_space=pltpu.SMEM)
    rows = parts[0].shape[0]
    return pl.pallas_call(
        finish_kernel,
        out_shape=jax.ShapeDtypeStruct((rows, 2, 8 * WIN_DEV), F32),
        in_specs=[sm, sm] + [vm] * 4,
        out_specs=vm,
        name="finish",
    )(core, place, *parts)


def step(c_occ, c_vir, e_occ, e_vir, tau_points, pair_blocks, block_count, three_center):
    y, z, c = lax.axis_index("yh"), lax.axis_index("z"), lax.axis_index("c")
    yl, x = lax.axis_index("yl"), lax.axis_index("x")
    group = (y * 4 + z) * 2 + c
    aux_rows = three_center.shape[0]
    chip_rows = aux_rows // 8

    window = jnp.transpose(three_center[:WIN_DEV], (1, 0, 2))
    near = [window] + [lax.ppermute(window, ZY, shift_zy(i)) for i in range(1, 8)]
    windows = near + [lax.ppermute(piece, "c", SWAP) for piece in near]

    facts = jnp.concatenate([pair_blocks.reshape(-1), block_count])
    facts = jnp.pad(facts, (0, 128 - facts.shape[0]))
    facts = jnp.broadcast_to(facts[None], (8, 128))
    facts = spread(facts, PAIR, 16)
    facts = facts[:, 0]
    names = facts[:, :2 * OWN].reshape(16 * OWN, 2)
    counts = facts[:, 2 * OWN]

    groups = jnp.arange(16, dtype=jnp.int32)
    before = jnp.sum(jnp.where(groups[None, :] < groups[:, None], counts[None, :], 0), axis=1)
    slots = jnp.arange(16 * OWN, dtype=jnp.int32)
    slot_in = slots % OWN
    slot_rank = jnp.where(
        slot_in < jnp.repeat(counts, OWN), jnp.repeat(before, OWN) + slot_in, -1)
    chosen = jnp.arange(LIVE, dtype=jnp.int32)[:, None] == slot_rank[None, :]
    sg = slots // OWN
    place_of = (
        jnp.where(sg % 2 == c, 0, 8 * OWN)
        + (((y - sg // 8) % 2) * 4 + (z - (sg // 2) % 4) % 4) * OWN + slot_in)
    where = jnp.sum(jnp.where(chosen, place_of[None, :], 0), axis=1)
    live_names = jnp.sum(jnp.where(chosen[:, :, None], names[None], 0), axis=1)

    local = jnp.arange(c_occ.shape[0], dtype=jnp.int32)
    wanted = live_names[:, None, :] * BS + jnp.arange(BS, dtype=jnp.int32)[None, :, None]
    wanted = wanted.reshape(LIVE * BS, 2) - group * c_occ.shape[0]
    pick_occ = (wanted[:, :1] == local[None, :]).astype(BF16)
    pick_vir = (wanted[:, 1:] == local[None, :]).astype(BF16)
    rows = jnp.concatenate(
        [
            jnp.dot(pick_occ, c_occ, preferred_element_type=F32).astype(BF16),
            jnp.dot(pick_vir, c_vir, preferred_element_type=F32).astype(BF16),
        ], axis=1)
    n_occ = c_occ.shape[1]
    n_half = rows.shape[1] // 2
    kept = jnp.where(c == 0, rows[:, :n_half], rows[:, n_half:])
    given = jnp.where(c == 0, rows[:, n_half:], rows[:, :n_half])
    base_own = lax.dynamic_index_in_dim(before, group, 0, keepdims=False)
    base_next = lax.dynamic_index_in_dim(before, group + 1 - 2 * c, 0, keepdims=False)
    given = lax.ppermute(given, "c", SWAP)
    given, base_own, base_next = lax.optimization_barrier((given, base_own, base_next))
    kept = kept + given
    kept = lax.all_to_all(kept.reshape(8, -1, n_half), ZY, 0, 0)
    kept = jnp.sum(kept.astype(F32), axis=0).astype(BF16)
    kept = spread(kept, ZY, 8).reshape(LIVE * BS, n_half)
    given = lax.ppermute(kept, "c", SWAP)
    rows = jnp.concatenate(
        [jnp.where(c == 0, kept, given), jnp.where(c == 0, given, kept)], axis=1)

    tau = jnp.where(c == 0, tau_points[0], tau_points[1])
    factor = jnp.concatenate([jnp.exp(tau * e_occ / 2.0), jnp.exp(-tau * e_vir / 2.0)])
    scaled = (rows.astype(F32) * factor[None, :]).astype(BF16)
    padded = jnp.concatenate([scaled, jnp.zeros((OWN * BS, scaled.shape[1]), BF16)], axis=0)
    own = jnp.concatenate(
        [
            lax.dynamic_slice_in_dim(padded, base_own * BS, OWN * BS, 0),
            lax.dynamic_slice_in_dim(padded, base_next * BS, OWN * BS, 0),
        ], axis=0)
    numbers = (((1,), (1,)), ((), ()))
    grams = jnp.stack(
        [
            lax.dot_general(own[:, :n_occ], scaled[:, :n_occ], numbers, preferred_element_type=F32),
            lax.dot_general(own[:, n_occ:], scaled[:, n_occ:], numbers, preferred_element_type=F32),
        ])
    grams = grams.reshape(2, CHIP, BS, LIVE * BS).transpose(1, 0, 2, 3)
    grams, three_center = lax.optimization_barrier((grams, three_center))
    mine = three_center.reshape(aux_rows, OWN * TILE)
    other = lax.ppermute(mine, "c", SWAP)
    grams = jnp.sum(lax.all_to_all(grams, AUX, 0, 0), axis=0)
    grams = grams.astype(BF16)
    tiles = spread(grams, AUX, 8)

    bounds = jnp.stack([
        lax.dynamic_index_in_dim(counts, group, 0, keepdims=False),
        lax.dynamic_index_in_dim(counts, group + 1 - 2 * c, 0, keepdims=False)])
    moved = moved_blocks(where, bounds, tiles, windows)

    by = lax.ppermute(moved, "yl", SWAP)
    bp = lax.ppermute(moved, "x", XP)
    bm = lax.ppermute(moved, "x", XM)
    byp = lax.ppermute(by, "x", XP)
    bym = lax.ppermute(by, "x", XM)
    bpp = lax.ppermute(bp, "x", XP)
    order = (6, 2, 5, 7, 1, 3, 4, 0)
    dests = jnp.stack([((y + i // 4) % 2) * 4 + (z + i % 4) % 4 for i in order]).astype(jnp.int32)
    partials = [partial_rows(dests, mine, other, [moved, by, bp, bm])]
    bym, partials[0] = lax.optimization_barrier((bym, partials[0]))
    bymm = lax.ppermute(bym, "x", XM)
    partials.append(partial_rows(dests, mine, other, [byp, bym, bpp, bymm]))
    yo = 1 - yl
    xp, xm, x2 = (x - 1) % 4, (x + 1) % 4, (x + 2) % 4
    place = jnp.stack([yl * 4 + x, yo * 4 + x, yl * 4 + xp, yl * 4 + xm,
                       yo * 4 + xp, yo * 4 + xm, yl * 4 + x2, yo * 4 + x2]).astype(jnp.int32)
    rows_dev = chip_rows // 2
    ends = []
    for partial in partials:
        sums = []
        for i, part in zip(order, partial):
            sums.append(lax.ppermute(part, ZY, shift_zy(i)) if i else part)
        leave = sum(lax.dynamic_slice_in_dim(part, (1 - c) * rows_dev, rows_dev, 0).astype(F32)
                    for part in sums)
        leave, *sums = lax.optimization_barrier((leave, *sums))
        stay = sum(lax.dynamic_slice_in_dim(part, c * rows_dev, rows_dev, 0).astype(F32)
                   for part in sums)
        ends += [stay, lax.ppermute(leave, "c", SWAP)]
    return finish(c.astype(jnp.int32).reshape(1), place, ends)


def solution(mesh):
    inner = Mesh(mesh.devices.reshape(2, 4, 2, 2, 4), ("yh", "z", "c", "yl", "x"))
    placed = (
        P(PAIR, AUX),
        P(PAIR, AUX),
        P(AUX),
        P(AUX),
        P(),
        P(PAIR, None),
        P(PAIR),
        P(AUX, PAIR, None),
    )
    return jax.shard_map(
        step,
        mesh=inner,
        in_specs=placed,
        out_specs=P(AUX + PAIR, None, None),
        check_vma=False,
    )
```

```python
import jax
import jax.numpy as jnp
from jax import lax
from jax.experimental import pallas as pl
from jax.experimental.pallas import tpu as pltpu
from jax.sharding import Mesh, PartitionSpec as P

BS = 16
TILE = BS * BS
WIN_DEV = 128
LIVE = 40
OWN = 4
CHIP = 2 * OWN
PAIR = ("yh", "z", "c")
ZY = ("yh", "z")
AUX = ("yl", "x")
SWAP = [(0, 1), (1, 0)]
XP = [(i, (i + 1) % 4) for i in range(4)]
XM = [(i, (i - 1) % 4) for i in range(4)]
F32 = jnp.float32
BF16 = jnp.bfloat16


def shift_zy(i):
    return [(y * 4 + z, ((y + i // 4) % 2) * 4 + (z + i % 4) % 4) for y in range(2) for z in range(4)]


def spread(x, axes, count):
    return lax.all_to_all(jnp.broadcast_to(x[None], (count,) + x.shape), axes, 0, 0)


def moved_kernel(where_ref, bound_ref, tiles_ref, *refs):
    pieces = refs[:16]
    out_ref, acc_ref, eo_ref, ev_ref, oe_ref, ve_ref, win_ref, all_ref, sems = refs[16:]
    copies = [
        pltpu.make_async_copy(piece, all_ref.at[pl.ds(n * OWN, OWN)], sems.at[n])
        for n, piece in enumerate(pieces)
    ]
    for copy in copies:
        copy.start()
    lane = lax.broadcasted_iota(jnp.int32, (128, 2048), 1)
    row = lax.broadcasted_iota(jnp.int32, (128, 2048), 0)
    block = (lane // TILE) * BS
    eo_ref[...] = (row == block + (lane % TILE) // BS).astype(BF16)
    ev_ref[...] = (row == block + lane % BS).astype(BF16)
    acc_ref[...] = jnp.zeros_like(acc_ref)
    for copy in copies:
        copy.wait()

    def group(g, carry):
        at = pl.multiple_of(g * 128, 128)
        occ = tiles_ref[:, 0, :, pl.ds(at, 128)].reshape(128, 128)
        vir = tiles_ref[:, 1, :, pl.ds(at, 128)].reshape(128, 128)
        numbers = (((0,), (0,)), ((), ()))
        oe_ref[...] = lax.dot_general(occ, eo_ref[...], numbers, preferred_element_type=F32)
        ve_ref[...] = lax.dot_general(vir, ev_ref[...], numbers, preferred_element_type=F32)
        for r in range(8):
            win_ref[r] = all_ref[where_ref[g * 8 + r]]

        def target(s, c):
            at = pl.multiple_of(s * TILE, TILE)
            total = acc_ref[s]
            for r in range(8):
                v = ve_ref[r * BS:(r + 1) * BS, pl.ds(at, TILE)]
                kron = jnp.concatenate(
                    [
                        (oe_ref[r * BS + j:r * BS + j + 1, pl.ds(at, TILE)] * v).astype(BF16)
                        for j in range(BS)
                    ], axis=0)
                total = total + jnp.dot(win_ref[r], kron, preferred_element_type=F32)
            acc_ref[s] = total
            return c

        return lax.fori_loop(0, CHIP, target, carry, unroll=4)

    lax.fori_loop(0, LIVE // 8, group, 0)
    for s in range(CHIP):
        live = s % OWN < bound_ref[s // OWN]
        out_ref[s * TILE:(s + 1) * TILE] = jnp.where(live, acc_ref[s].T, 0.0).astype(BF16)


def moved_blocks(where, bounds, tiles, pieces):
    vm = pl.BlockSpec(memory_space=pltpu.VMEM)
    sm = pl.BlockSpec(memory_space=pltpu.SMEM)
    return pl.pallas_call(
        moved_kernel,
        out_shape=jax.ShapeDtypeStruct((CHIP * TILE, WIN_DEV), BF16),
        in_specs=[sm, sm, vm] + [pl.BlockSpec(memory_space=pl.ANY)] * 16,
        out_specs=vm,
        scratch_shapes=[
            pltpu.VMEM((CHIP, WIN_DEV, TILE), F32),
            pltpu.VMEM((128, 2048), BF16),
            pltpu.VMEM((128, 2048), BF16),
            pltpu.VMEM((128, 2048), F32),
            pltpu.VMEM((128, 2048), F32),
            pltpu.VMEM((8, WIN_DEV, TILE), BF16),
            pltpu.VMEM((16 * OWN, WIN_DEV, TILE), BF16),
            pltpu.SemaphoreType.DMA((16,)),
        ],
        name="moved",
    )(where, bounds, tiles, *pieces)


def partial_kernel(dest_ref, mine_ref, other_ref, *refs):
    half = OWN * TILE
    outs = refs[-8:]
    refs = list(refs[:-8])
    step = pl.program_id(0)
    tops = [ref[:half] for ref in refs]
    bots = [ref[half:] for ref in refs]
    values = []
    for n in range(0, len(tops), 2):
        top = jnp.concatenate(tops[n:n + 2], axis=1)
        bot = jnp.concatenate(bots[n:n + 2], axis=1)
        value = jnp.dot(mine_ref[...], top, preferred_element_type=F32)
        value = value + jnp.dot(other_ref[...], bot, preferred_element_type=F32)
        values.append(value.astype(BF16))
    value = jnp.concatenate(values, axis=1)
    rows = outs[0].shape[0]
    for k, out_ref in enumerate(outs):
        for h in range(2):
            @pl.when(dest_ref[k] == 2 * step + h)
            def _():
                out_ref[...] = value[h * rows:(h + 1) * rows]


def partial_rows(dests, mine, other, pieces):
    rows = mine.shape[0] // 8
    a_spec = pl.BlockSpec((2 * rows, mine.shape[1]), lambda i, d: (i, 0))
    vm = pl.BlockSpec(memory_space=pltpu.VMEM)
    return pl.pallas_call(
        partial_kernel,
        out_shape=[jax.ShapeDtypeStruct((rows, 4 * WIN_DEV), BF16)] * 8,
        grid_spec=pltpu.PrefetchScalarGridSpec(
            num_scalar_prefetch=1,
            grid=(4,),
            in_specs=[a_spec, a_spec] + [vm] * len(pieces),
            out_specs=[vm] * 8,
        ),
        name="partial",
    )(dests, mine, other, *pieces)


def finish_kernel(core_ref, place_ref, *refs):
    out_ref = refs[-1]
    first = core_ref[0] == 0
    for b in range(8):
        stay, came = refs[2 * (b // 4)], refs[2 * (b // 4) + 1]
        at = slice((b % 4) * WIN_DEV, (b % 4 + 1) * WIN_DEV)
        s, r = stay[:, at], came[:, at]
        to = pl.multiple_of(place_ref[b] * WIN_DEV, WIN_DEV)
        out_ref[:, 0, pl.ds(to, WIN_DEV)] = jnp.where(first, s, r)
        out_ref[:, 1, pl.ds(to, WIN_DEV)] = jnp.where(first, r, s)


def finish(core, place, parts):
    vm = pl.BlockSpec(memory_space=pltpu.VMEM)
    sm = pl.BlockSpec(memory_space=pltpu.SMEM)
    rows = parts[0].shape[0]
    return pl.pallas_call(
        finish_kernel,
        out_shape=jax.ShapeDtypeStruct((rows, 2, 8 * WIN_DEV), F32),
        in_specs=[sm, sm] + [vm] * 4,
        out_specs=vm,
        name="finish",
    )(core, place, *parts)


def step(c_occ, c_vir, e_occ, e_vir, tau_points, pair_blocks, block_count, three_center):
    y, z, c = lax.axis_index("yh"), lax.axis_index("z"), lax.axis_index("c")
    yl, x = lax.axis_index("yl"), lax.axis_index("x")
    group = (y * 4 + z) * 2 + c
    aux_rows = three_center.shape[0]
    chip_rows = aux_rows // 8

    facts = jnp.concatenate([pair_blocks.reshape(-1), block_count])
    facts = jnp.pad(facts, (0, 128 - facts.shape[0]))
    facts = jnp.broadcast_to(facts[None], (8, 128))
    facts = spread(facts, PAIR, 16)
    facts = facts[:, 0]
    names = facts[:, :2 * OWN].reshape(16 * OWN, 2)
    counts = facts[:, 2 * OWN]

    groups = jnp.arange(16, dtype=jnp.int32)
    before = jnp.sum(jnp.where(groups[None, :] < groups[:, None], counts[None, :], 0), axis=1)
    slots = jnp.arange(16 * OWN, dtype=jnp.int32)
    slot_in = slots % OWN
    slot_rank = jnp.where(
        slot_in < jnp.repeat(counts, OWN), jnp.repeat(before, OWN) + slot_in, -1)
    chosen = jnp.arange(LIVE, dtype=jnp.int32)[:, None] == slot_rank[None, :]
    sg = slots // OWN
    place_of = (
        jnp.where(sg % 2 == c, 0, 8 * OWN)
        + (((y - sg // 8) % 2) * 4 + (z - (sg // 2) % 4) % 4) * OWN + slot_in)
    where = jnp.sum(jnp.where(chosen, place_of[None, :], 0), axis=1)
    live_names = jnp.sum(jnp.where(chosen[:, :, None], names[None], 0), axis=1)

    local = jnp.arange(c_occ.shape[0], dtype=jnp.int32)
    wanted = live_names[:, None, :] * BS + jnp.arange(BS, dtype=jnp.int32)[None, :, None]
    wanted = wanted.reshape(LIVE * BS, 2) - group * c_occ.shape[0]
    pick_occ = (wanted[:, :1] == local[None, :]).astype(BF16)
    pick_vir = (wanted[:, 1:] == local[None, :]).astype(BF16)
    rows = jnp.concatenate(
        [
            jnp.dot(pick_occ, c_occ, preferred_element_type=F32).astype(BF16),
            jnp.dot(pick_vir, c_vir, preferred_element_type=F32).astype(BF16),
        ], axis=1)
    n_occ = c_occ.shape[1]
    n_half = rows.shape[1] // 2
    kept = jnp.where(c == 0, rows[:, :n_half], rows[:, n_half:])
    given = jnp.where(c == 0, rows[:, n_half:], rows[:, :n_half])
    base_own = lax.dynamic_index_in_dim(before, group, 0, keepdims=False)
    base_next = lax.dynamic_index_in_dim(before, group + 1 - 2 * c, 0, keepdims=False)
    given = lax.ppermute(given, "c", SWAP)
    yo = 1 - yl
    xp, xm, x2 = (x - 1) % 4, (x + 1) % 4, (x + 2) % 4
    place = jnp.stack([yl * 4 + x, yo * 4 + x, yl * 4 + xp, yl * 4 + xm,
                       yo * 4 + xp, yo * 4 + xm, yl * 4 + x2, yo * 4 + x2]).astype(jnp.int32)
    order = (6, 2, 5, 7, 1, 3, 4, 0)
    dests = jnp.stack([((y + i // 4) % 2) * 4 + (z + i % 4) % 4 for i in order]).astype(jnp.int32)
    given, base_own, base_next, place, dests = lax.optimization_barrier(
        (given, base_own, base_next, place, dests))
    kept = kept + given
    kept = lax.all_to_all(kept.reshape(8, -1, n_half), ZY, 0, 0)
    mine = three_center.reshape(aux_rows, OWN * TILE)
    window = jnp.transpose(three_center[:WIN_DEV], (1, 0, 2))
    tau = jnp.sum(jnp.where(jnp.arange(2) == c, tau_points, 0.0), keepdims=True)
    kept, mine, window, tau = lax.optimization_barrier((kept, mine, window, tau))
    near = [window] + [lax.ppermute(window, ZY, shift_zy(i)) for i in range(1, 8)]
    windows = near + [lax.ppermute(piece, "c", SWAP) for piece in near]
    kept = jnp.sum(kept.astype(F32), axis=0).astype(BF16)
    kept = spread(kept, ZY, 8).reshape(LIVE * BS, n_half)
    given = lax.ppermute(kept, "c", SWAP)
    rows = jnp.concatenate(
        [jnp.where(c == 0, kept, given), jnp.where(c == 0, given, kept)], axis=1)

    factor = jnp.concatenate([jnp.exp(tau * e_occ / 2.0), jnp.exp(-tau * e_vir / 2.0)])
    scaled = (rows.astype(F32) * factor[None, :]).astype(BF16)
    padded = jnp.concatenate([scaled, jnp.zeros((OWN * BS, scaled.shape[1]), BF16)], axis=0)
    own = jnp.concatenate(
        [
            lax.dynamic_slice_in_dim(padded, base_own * BS, OWN * BS, 0),
            lax.dynamic_slice_in_dim(padded, base_next * BS, OWN * BS, 0),
        ], axis=0)
    numbers = (((1,), (1,)), ((), ()))
    grams = jnp.stack(
        [
            lax.dot_general(own[:, :n_occ], scaled[:, :n_occ], numbers, preferred_element_type=F32),
            lax.dot_general(own[:, n_occ:], scaled[:, n_occ:], numbers, preferred_element_type=F32),
        ])
    grams = grams.reshape(2, CHIP, BS, LIVE * BS).transpose(1, 0, 2, 3)
    grams = jnp.sum(lax.all_to_all(grams, AUX, 0, 0), axis=0)
    grams = grams.astype(BF16)
    grams, mine = lax.optimization_barrier((grams, mine))
    other = lax.ppermute(mine, "c", SWAP)
    tiles = spread(grams, AUX, 8)

    bounds = jnp.stack([
        lax.dynamic_index_in_dim(counts, group, 0, keepdims=False),
        lax.dynamic_index_in_dim(counts, group + 1 - 2 * c, 0, keepdims=False)])
    moved = moved_blocks(where, bounds, tiles, windows)

    by = lax.ppermute(moved, "yl", SWAP)
    bp = lax.ppermute(moved, "x", XP)
    bm = lax.ppermute(moved, "x", XM)
    byp = lax.ppermute(by, "x", XP)
    bym = lax.ppermute(by, "x", XM)
    bpp = lax.ppermute(bp, "x", XP)
    partials = [partial_rows(dests, mine, other, [moved, by, bp, bm])]
    bym, partials[0] = lax.optimization_barrier((bym, partials[0]))
    bymm = lax.ppermute(bym, "x", XM)
    partials.append(partial_rows(dests, mine, other, [byp, bym, bpp, bymm]))
    rows_dev = chip_rows // 2
    ends = []
    for partial in partials:
        sums = []
        for i, part in zip(order, partial):
            sums.append(lax.ppermute(part, ZY, shift_zy(i)) if i else part)

        def half_of(which, picked):
            return sum(
                lax.dynamic_slice_in_dim(part, which * rows_dev, rows_dev, 0).astype(F32)
                for i, part in zip(order, sums) if picked(i))

        leave, stay = lax.optimization_barrier(
            (half_of(1 - c, lambda i: i < 4), half_of(c, lambda i: i < 4)))
        leave = leave + half_of(1 - c, lambda i: i >= 4)
        leave, stay, *sums = lax.optimization_barrier((leave, stay, *sums))
        stay = stay + half_of(c, lambda i: i >= 4)
        ends += [stay, lax.ppermute(leave, "c", SWAP)]
    return finish(c.astype(jnp.int32).reshape(1), place, ends)


def solution(mesh):
    inner = Mesh(mesh.devices.reshape(2, 4, 2, 2, 4), ("yh", "z", "c", "yl", "x"))
    placed = (
        P(PAIR, AUX),
        P(PAIR, AUX),
        P(AUX),
        P(AUX),
        P(),
        P(PAIR, None),
        P(PAIR),
        P(AUX, PAIR, None),
    )
    return jax.shard_map(
        step,
        mesh=inner,
        in_specs=placed,
        out_specs=P(AUX + PAIR, None, None),
        check_vma=False,
    )
```

```python
import jax
import jax.numpy as jnp
from jax import lax
from jax.experimental import pallas as pl
from jax.experimental.pallas import tpu as pltpu
from jax.sharding import Mesh, PartitionSpec as P

BS = 16
TILE = BS * BS
WIN_DEV = 128
LIVE = 40
OWN = 4
CHIP = 2 * OWN
PAIR = ("yh", "z", "c")
ZY = ("yh", "z")
AUX = ("yl", "x")
SWAP = [(0, 1), (1, 0)]
XP = [(i, (i + 1) % 4) for i in range(4)]
XM = [(i, (i - 1) % 4) for i in range(4)]
F32 = jnp.float32
BF16 = jnp.bfloat16


def shift_zy(i):
    return [(y * 4 + z, ((y + i // 4) % 2) * 4 + (z + i % 4) % 4) for y in range(2) for z in range(4)]


def spread(x, axes, count):
    return lax.all_to_all(jnp.broadcast_to(x[None], (count,) + x.shape), axes, 0, 0)


def moved_kernel(where_ref, bound_ref, tiles_ref, *refs):
    pieces = refs[:8]
    out_ref, acc_ref, eo_ref, ev_ref, oe_ref, ve_ref, win_ref, all_ref, sems = refs[8:]
    copies = [
        pltpu.make_async_copy(piece, all_ref.at[pl.ds(n * CHIP, CHIP)], sems.at[n])
        for n, piece in enumerate(pieces)
    ]
    for copy in copies:
        copy.start()
    lane = lax.broadcasted_iota(jnp.int32, (128, 2048), 1)
    row = lax.broadcasted_iota(jnp.int32, (128, 2048), 0)
    block = (lane // TILE) * BS
    eo_ref[...] = (row == block + (lane % TILE) // BS).astype(BF16)
    ev_ref[...] = (row == block + lane % BS).astype(BF16)
    acc_ref[...] = jnp.zeros_like(acc_ref)
    for copy in copies:
        copy.wait()

    def group(g, carry):
        at = pl.multiple_of(g * 128, 128)
        occ = tiles_ref[:, 0, :, pl.ds(at, 128)].reshape(128, 128)
        vir = tiles_ref[:, 1, :, pl.ds(at, 128)].reshape(128, 128)
        numbers = (((0,), (0,)), ((), ()))
        oe_ref[...] = lax.dot_general(occ, eo_ref[...], numbers, preferred_element_type=F32)
        ve_ref[...] = lax.dot_general(vir, ev_ref[...], numbers, preferred_element_type=F32)
        for r in range(8):
            win_ref[r] = all_ref[where_ref[g * 8 + r]]

        def target(s, c):
            at = pl.multiple_of(s * TILE, TILE)
            total = acc_ref[s]
            for r in range(8):
                v = ve_ref[r * BS:(r + 1) * BS, pl.ds(at, TILE)]
                kron = jnp.concatenate(
                    [
                        (oe_ref[r * BS + j:r * BS + j + 1, pl.ds(at, TILE)] * v).astype(BF16)
                        for j in range(BS)
                    ], axis=0)
                total = total + jnp.dot(win_ref[r], kron, preferred_element_type=F32)
            acc_ref[s] = total
            return c

        return lax.fori_loop(0, CHIP, target, carry, unroll=8)

    lax.fori_loop(0, LIVE // 8, group, 0)
    for s in range(CHIP):
        live = s % OWN < bound_ref[s // OWN]
        out_ref[s * TILE:(s + 1) * TILE] = jnp.where(live, acc_ref[s].T, 0.0).astype(BF16)


def moved_blocks(where, bounds, tiles, pieces):
    vm = pl.BlockSpec(memory_space=pltpu.VMEM)
    sm = pl.BlockSpec(memory_space=pltpu.SMEM)
    return pl.pallas_call(
        moved_kernel,
        out_shape=jax.ShapeDtypeStruct((CHIP * TILE, WIN_DEV), BF16),
        in_specs=[sm, sm, vm] + [pl.BlockSpec(memory_space=pl.ANY)] * 8,
        out_specs=vm,
        scratch_shapes=[
            pltpu.VMEM((CHIP, WIN_DEV, TILE), F32),
            pltpu.VMEM((128, 2048), BF16),
            pltpu.VMEM((128, 2048), BF16),
            pltpu.VMEM((128, 2048), F32),
            pltpu.VMEM((128, 2048), F32),
            pltpu.VMEM((8, WIN_DEV, TILE), BF16),
            pltpu.VMEM((16 * OWN, WIN_DEV, TILE), BF16),
            pltpu.SemaphoreType.DMA((8,)),
        ],
        name="moved",
    )(where, bounds, tiles, *pieces)


def partial_kernel(dest_ref, mine_ref, other_ref, *refs):
    half = OWN * TILE
    outs = refs[-8:]
    refs = list(refs[:-8])
    step = pl.program_id(0)
    tops = [ref[:half] for ref in refs]
    bots = [ref[half:] for ref in refs]
    values = []
    for n in range(0, len(tops), 2):
        top = jnp.concatenate(tops[n:n + 2], axis=1)
        bot = jnp.concatenate(bots[n:n + 2], axis=1)
        value = jnp.dot(mine_ref[...], top, preferred_element_type=F32)
        value = value + jnp.dot(other_ref[...], bot, preferred_element_type=F32)
        values.append(value.astype(BF16))
    value = jnp.concatenate(values, axis=1)
    rows = outs[0].shape[0]
    for k, out_ref in enumerate(outs):
        for h in range(2):
            @pl.when(dest_ref[k] == 2 * step + h)
            def _():
                out_ref[...] = value[h * rows:(h + 1) * rows]


def partial_rows(dests, mine, other, pieces):
    rows = mine.shape[0] // 8
    a_spec = pl.BlockSpec((2 * rows, mine.shape[1]), lambda i, d: (i, 0))
    vm = pl.BlockSpec(memory_space=pltpu.VMEM)
    return pl.pallas_call(
        partial_kernel,
        out_shape=[jax.ShapeDtypeStruct((rows, 4 * WIN_DEV), BF16)] * 8,
        grid_spec=pltpu.PrefetchScalarGridSpec(
            num_scalar_prefetch=1,
            grid=(4,),
            in_specs=[a_spec, a_spec] + [vm] * len(pieces),
            out_specs=[vm] * 8,
        ),
        name="partial",
    )(dests, mine, other, *pieces)


def finish_kernel(core_ref, place_ref, *refs):
    out_ref = refs[-1]
    first = core_ref[0] == 0
    for b in range(8):
        stay, came = refs[2 * (b // 4)], refs[2 * (b // 4) + 1]
        at = slice((b % 4) * WIN_DEV, (b % 4 + 1) * WIN_DEV)
        s, r = stay[:, at], came[:, at]
        to = pl.multiple_of(place_ref[b] * WIN_DEV, WIN_DEV)
        out_ref[:, 0, pl.ds(to, WIN_DEV)] = jnp.where(first, s, r)
        out_ref[:, 1, pl.ds(to, WIN_DEV)] = jnp.where(first, r, s)


def finish(core, place, parts):
    vm = pl.BlockSpec(memory_space=pltpu.VMEM)
    sm = pl.BlockSpec(memory_space=pltpu.SMEM)
    rows = parts[0].shape[0]
    return pl.pallas_call(
        finish_kernel,
        out_shape=jax.ShapeDtypeStruct((rows, 2, 8 * WIN_DEV), F32),
        in_specs=[sm, sm] + [vm] * 4,
        out_specs=vm,
        name="finish",
    )(core, place, *parts)


def step(c_occ, c_vir, e_occ, e_vir, tau_points, pair_blocks, block_count, three_center):
    y, z, c = lax.axis_index("yh"), lax.axis_index("z"), lax.axis_index("c")
    yl, x = lax.axis_index("yl"), lax.axis_index("x")
    group = (y * 4 + z) * 2 + c
    aux_rows = three_center.shape[0]
    chip_rows = aux_rows // 8

    window = jnp.transpose(three_center[:WIN_DEV], (1, 0, 2))
    paired = lax.ppermute(window, "yh", SWAP)
    facts = jnp.concatenate([pair_blocks.reshape(-1), block_count])
    facts = jnp.pad(facts, (0, 128 - facts.shape[0]))
    facts = jnp.broadcast_to(facts[None], (8, 128))
    facts = spread(facts, PAIR, 16)
    facts = facts[:, 0]
    names = facts[:, :2 * OWN].reshape(16 * OWN, 2)
    counts = facts[:, 2 * OWN]

    groups = jnp.arange(16, dtype=jnp.int32)
    before = jnp.sum(jnp.where(groups[None, :] < groups[:, None], counts[None, :], 0), axis=1)
    slots = jnp.arange(16 * OWN, dtype=jnp.int32)
    slot_in = slots % OWN
    slot_rank = jnp.where(
        slot_in < jnp.repeat(counts, OWN), jnp.repeat(before, OWN) + slot_in, -1)
    chosen = jnp.arange(LIVE, dtype=jnp.int32)[:, None] == slot_rank[None, :]
    sg = slots // OWN
    place_of = (
        jnp.where(sg % 2 == c, 0, 8 * OWN) + ((z - (sg // 2) % 4) % 4) * CHIP
        + jnp.where(sg // 8 == y, 0, OWN) + slot_in)
    where = jnp.sum(jnp.where(chosen, place_of[None, :], 0), axis=1)
    live_names = jnp.sum(jnp.where(chosen[:, :, None], names[None], 0), axis=1)

    local = jnp.arange(c_occ.shape[0], dtype=jnp.int32)
    wanted = live_names[:, None, :] * BS + jnp.arange(BS, dtype=jnp.int32)[None, :, None]
    wanted = wanted.reshape(LIVE * BS, 2) - group * c_occ.shape[0]
    pick_occ = (wanted[:, :1] == local[None, :]).astype(BF16)
    pick_vir = (wanted[:, 1:] == local[None, :]).astype(BF16)
    rows = jnp.concatenate(
        [
            jnp.dot(pick_occ, c_occ, preferred_element_type=F32).astype(BF16),
            jnp.dot(pick_vir, c_vir, preferred_element_type=F32).astype(BF16),
        ], axis=1)
    n_occ = c_occ.shape[1]
    n_half = rows.shape[1] // 2
    kept = jnp.where(c == 0, rows[:, :n_half], rows[:, n_half:])
    given = jnp.where(c == 0, rows[:, n_half:], rows[:, :n_half])
    base_own = lax.dynamic_index_in_dim(before, group, 0, keepdims=False)
    base_next = lax.dynamic_index_in_dim(before, group + 1 - 2 * c, 0, keepdims=False)
    given = lax.ppermute(given, "c", SWAP)
    yo = 1 - yl
    xp, xm, x2 = (x - 1) % 4, (x + 1) % 4, (x + 2) % 4
    place = jnp.stack([yl * 4 + x, yo * 4 + x, yl * 4 + xp, yl * 4 + xm,
                       yo * 4 + xp, yo * 4 + xm, yl * 4 + x2, yo * 4 + x2]).astype(jnp.int32)
    order = (6, 2, 5, 7, 1, 3, 4, 0)
    dests = jnp.stack([((y + i // 4) % 2) * 4 + (z + i % 4) % 4 for i in order]).astype(jnp.int32)
    given, base_own, base_next, place, dests = lax.optimization_barrier(
        (given, base_own, base_next, place, dests))
    kept = kept + given
    kept = lax.all_to_all(kept.reshape(8, -1, n_half), ZY, 0, 0)
    mine = three_center.reshape(aux_rows, OWN * TILE)
    tau = jnp.sum(jnp.where(jnp.arange(2) == c, tau_points, 0.0), keepdims=True)
    packed = jnp.concatenate([window, paired])
    kept, mine, packed, tau = lax.optimization_barrier((kept, mine, packed, tau))
    near = [packed] + [
        lax.ppermute(packed, "z", [(n, (n + i) % 4) for n in range(4)]) for i in range(1, 4)]
    windows = near + [lax.ppermute(piece, "c", SWAP) for piece in near]
    kept = jnp.sum(kept.astype(F32), axis=0).astype(BF16)
    kept = spread(kept, ZY, 8).reshape(LIVE * BS, n_half)
    given = lax.ppermute(kept, "c", SWAP)
    rows = jnp.concatenate(
        [jnp.where(c == 0, kept, given), jnp.where(c == 0, given, kept)], axis=1)

    factor = jnp.concatenate([jnp.exp(tau * e_occ / 2.0), jnp.exp(-tau * e_vir / 2.0)])
    scaled = (rows.astype(F32) * factor[None, :]).astype(BF16)
    padded = jnp.concatenate([scaled, jnp.zeros((OWN * BS, scaled.shape[1]), BF16)], axis=0)
    own = jnp.concatenate(
        [
            lax.dynamic_slice_in_dim(padded, base_own * BS, OWN * BS, 0),
            lax.dynamic_slice_in_dim(padded, base_next * BS, OWN * BS, 0),
        ], axis=0)
    numbers = (((1,), (1,)), ((), ()))
    grams = jnp.stack(
        [
            lax.dot_general(own[:, :n_occ], scaled[:, :n_occ], numbers, preferred_element_type=F32),
            lax.dot_general(own[:, n_occ:], scaled[:, n_occ:], numbers, preferred_element_type=F32),
        ])
    grams = grams.reshape(2, CHIP, BS, LIVE * BS).transpose(1, 0, 2, 3)
    grams = jnp.sum(lax.all_to_all(grams, AUX, 0, 0), axis=0)
    grams = grams.astype(BF16)
    grams, mine = lax.optimization_barrier((grams, mine))
    other = lax.ppermute(mine, "c", SWAP)
    tiles = spread(grams, AUX, 8)

    bounds = jnp.stack([
        lax.dynamic_index_in_dim(counts, group, 0, keepdims=False),
        lax.dynamic_index_in_dim(counts, group + 1 - 2 * c, 0, keepdims=False)])
    moved = moved_blocks(where, bounds, tiles, windows)

    by = lax.ppermute(moved, "yl", SWAP)
    bp = lax.ppermute(moved, "x", XP)
    bm = lax.ppermute(moved, "x", XM)
    byp = lax.ppermute(by, "x", XP)
    bym = lax.ppermute(by, "x", XM)
    bpp = lax.ppermute(bp, "x", XP)
    partials = [partial_rows(dests, mine, other, [moved, by, bp, bm])]
    bym, partials[0] = lax.optimization_barrier((bym, partials[0]))
    bymm = lax.ppermute(bym, "x", XM)
    partials.append(partial_rows(dests, mine, other, [byp, bym, bpp, bymm]))
    rows_dev = chip_rows // 2
    ends = []
    for partial in partials:
        sums = []
        for i, part in zip(order, partial):
            sums.append(lax.ppermute(part, ZY, shift_zy(i)) if i else part)

        def half_of(which, picked):
            return sum(
                lax.dynamic_slice_in_dim(part, which * rows_dev, rows_dev, 0).astype(F32)
                for i, part in zip(order, sums) if picked(i))

        leave, stay = lax.optimization_barrier(
            (half_of(1 - c, lambda i: i < 4), half_of(c, lambda i: i < 4)))
        leave = leave + half_of(1 - c, lambda i: i >= 4)
        leave, stay, *sums = lax.optimization_barrier((leave, stay, *sums))
        stay = stay + half_of(c, lambda i: i >= 4)
        ends += [stay, lax.ppermute(leave, "c", SWAP)]
    return finish(c.astype(jnp.int32).reshape(1), place, ends)


def solution(mesh):
    inner = Mesh(mesh.devices.reshape(2, 4, 2, 2, 4), ("yh", "z", "c", "yl", "x"))
    placed = (
        P(PAIR, AUX),
        P(PAIR, AUX),
        P(AUX),
        P(AUX),
        P(),
        P(PAIR, None),
        P(PAIR),
        P(AUX, PAIR, None),
    )
    return jax.shard_map(
        step,
        mesh=inner,
        in_specs=placed,
        out_specs=P(AUX + PAIR, None, None),
        check_vma=False,
    )
```
